32 devices in a mesh: dp: 16 (over z, y, core), rows: 2 (over x).
Axes of the slice: x: 2, y: 2, z: 4, core: 2. Of those that a mesh axis runs over, the one named last changes fastest.
Arguments:
- latents: bfloat16 [16, 4, 128, 320], P('dp', 'rows'), may hold values from -6 to 6
- mean_one: float32 [16, 32], P('dp'), may hold values from -0.5 to 0.5
- rstd_one: float32 [16, 32], P('dp'), may hold values from 0.5 to 2
- gain_one: float32 [320], replicated, may hold values from 0.25 to 1.75
- shift_one: float32 [320], replicated, may hold values from -0.5 to 0.5
- kernel_one: bfloat16 [4, 9, 25600], P(None, None, 'dp'), may hold values from -0.109375 to 0.109375
- bias_one: float32 [320], replicated, may hold values from -3 to 3
- embed_bias: float32 [16, 320], P('dp'), may hold values from -3 to 3
- mean_two: float32 [16, 32], P('dp'), may hold values from -0.5 to 0.5
- rstd_two: float32 [16, 32], P('dp'), may hold values from 0.5 to 2
- gain_two: float32 [320], replicated, may hold values from 0.25 to 1.75
- shift_two: float32 [320], replicated, may hold values from -0.5 to 0.5
- kernel_two: bfloat16 [4, 9, 25600], P(None, None, 'dp'), may hold values from -0.109375 to 0.109375
- bias_two: float32 [320], replicated, may hold values from -3 to 3
Outputs:
- block_out: bfloat16 [16, 4, 128, 320], P('dp', 'rows')
The draws below stay inside these ranges and needn't reach their ends.
All inputs are finite; a program needn't handle non-finite values.
Results may differ from the reference program's by a relative error of at most 0.0045.
Values may be sent and summed in bfloat16 or wider, within the bound.
No kernel may reach another device: no remote copies, remote signals or barrier semaphores. Data moves between devices by JAX's collectives and lax.ppermute only.
A program may use at most 192 MiB of HBM per device.

```python
import math
import jax
import jax.numpy as jnp
from jax import lax

C = 320
GROUPS = 32
SPANS = 4
COLS = 128
SPAN = 80
HEIGHT = 4
LATENTS = 16


def level_of(rng, extent, shards, least, high):
    loudness, own = 1.0, jax.random.fold_in(rng, 6)
    for dim, parts in shards:
        heights = jnp.exp(jax.random.uniform(jax.random.fold_in(own, dim), (parts,), jnp.float32, least / len(shards), high / len(shards)))
        loudness = loudness * jnp.repeat(heights, extent[dim] // parts).reshape([-1 if axis == dim else 1 for axis in range(len(extent))])
    return loudness


def bell_draw(own_key, dims, scale, bound, pieces=(), kind=jnp.bfloat16):
    values = scale * jax.random.normal(own_key, dims, jnp.float32)
    if pieces:
        values = values * level_of(own_key, dims, pieces, -0.22, 0.18)
    return jnp.clip(values, -bound, bound).astype(kind)


def setup_inputs(seed: int = 0) -> dict:
    key_of = jax.random.split(jax.random.key(seed), 15)
    return {
        "latents": bell_draw(key_of[0], (LATENTS, HEIGHT, COLS, C), 1.0, 6.0, ((0, 16), (1, 2))),
        "mean_one": jnp.clip(jax.random.uniform(key_of[1], (LATENTS, GROUPS), jnp.float32, -0.5, 0.5) * level_of(key_of[1], (LATENTS, GROUPS), ((0, 16),), -0.4, 0.0), -0.5, 0.5),
        "rstd_one": jnp.clip(jnp.exp(math.log(2.0) - 1.3862944 * jax.random.uniform(key_of[2], (LATENTS, GROUPS), jnp.float32) ** level_of(key_of[2], (LATENTS, GROUPS), ((0, 16),), -0.2, 0.2)), 0.5, 2.0),
        "gain_one": jnp.clip(1.0 + 0.15 * jax.random.normal(key_of[3], (C,), jnp.float32), 0.25, 1.75),
        "shift_one": jnp.clip(jax.random.uniform(key_of[4], (C,), jnp.float32, -0.5, 0.5), -0.5, 0.5),
        "kernel_one": bell_draw(key_of[5], (SPANS, 9, SPAN * C), (9 * C) ** -0.5, 0.109375, ((2, 16),)),
        "bias_one": bell_draw(key_of[6], (C,), 0.5, 3.0, (), jnp.float32),
        "embed_bias": bell_draw(key_of[7], (LATENTS, C), 0.5, 3.0, ((0, 16),), jnp.float32),
        "mean_two": jnp.clip(jax.random.uniform(key_of[8], (LATENTS, GROUPS), jnp.float32, -0.5, 0.5) * level_of(key_of[8], (LATENTS, GROUPS), ((0, 16),), -0.4, 0.0), -0.5, 0.5),
        "rstd_two": jnp.clip(jnp.exp(math.log(2.0) - 1.3862944 * jax.random.uniform(key_of[9], (LATENTS, GROUPS), jnp.float32) ** level_of(key_of[9], (LATENTS, GROUPS), ((0, 16),), -0.2, 0.2)), 0.5, 2.0),
        "gain_two": jnp.clip(1.0 + 0.15 * jax.random.normal(key_of[10], (C,), jnp.float32), 0.25, 1.75),
        "shift_two": jnp.clip(jax.random.uniform(key_of[11], (C,), jnp.float32, -0.5, 0.5), -0.5, 0.5),
        "kernel_two": bell_draw(key_of[12], (SPANS, 9, SPAN * C), (9 * C) ** -0.5, 0.109375, ((2, 16),)),
        "bias_two": bell_draw(key_of[13], (C,), 0.5, 3.0, (), jnp.float32),
    }


def norm_silu(values, group_mean, group_rstd, gain_vec, shift_vec):
    height, columns, channels = values.shape
    groups = group_mean.shape[0]
    grouped = values.reshape(height, columns, groups, channels // groups)
    scaled = (grouped - group_mean[:, None]) * group_rstd[:, None]
    return jax.nn.silu(scaled.reshape(height, columns, channels) * gain_vec + shift_vec)


def convolve(activation, kernel):
    channels = activation.shape[-1]
    blocks = kernel.shape[0]
    weights = kernel.astype(jnp.float32).reshape(blocks, 3, 3, channels // blocks, channels)
    weights = jnp.transpose(weights, (1, 2, 0, 3, 4)).reshape(3, 3, channels, channels)
    result = lax.conv_general_dilated(
        activation.astype(jnp.float32)[None], weights, (1, 1), ((1, 1), (1, 1)),
        dimension_numbers=("NHWC", "HWIO", "NHWC"), precision=lax.Precision.HIGHEST)
    return result[0]


def reference(latents, mean_one, rstd_one, gain_one, shift_one, kernel_one, bias_one, embed_bias,
              mean_two, rstd_two, gain_two, shift_two, kernel_two, bias_two):
    def one_latent(inputs):
        sample, first_mean, first_rstd, embedding, second_mean, second_rstd = inputs
        sample_f = sample.astype(jnp.float32)
        first_act = norm_silu(sample_f, first_mean, first_rstd, gain_one, shift_one).astype(jnp.bfloat16)
        hidden = convolve(first_act, kernel_one) + bias_one + embedding
        second_act = norm_silu(hidden, second_mean, second_rstd, gain_two, shift_two).astype(jnp.bfloat16)
        result = convolve(second_act, kernel_two) + bias_two + sample_f
        return result.astype(jnp.bfloat16)

    return lax.map(one_latent, (latents, mean_one, rstd_one, embed_bias, mean_two, rstd_two))
```

```python
import jax
import jax.numpy as jnp
from jax import lax
from jax.sharding import PartitionSpec as P


def padded_2(array, sides, width):
    for axis, dim in sides:
        devices, length = (lax.axis_size(axis), array.shape[dim])
        up = [(i, (i + 1) % devices) for i in range(devices - 1)]
        down = [(j, i) for i, j in up]
        last = lax.slice_in_dim(array, length - width, length, axis=dim)
        first = lax.slice_in_dim(array, 0, width, axis=dim)
        before = lax.ppermute(last, axis, up)
        after = lax.ppermute(first, axis, down)
        array = jnp.concatenate([before, array, after], axis=dim)
    return array


def norm_silu(values, group_mean, group_rstd, gain_vec, shift_vec):
    height, columns, channels = values.shape
    groups = group_mean.shape[-1]
    grouped = values.reshape(height, columns, groups, channels // groups)
    scaled = (grouped - group_mean[0][:, None]) * group_rstd[0][:, None]
    return jax.nn.silu(scaled.reshape(height, columns, channels) * gain_vec + shift_vec)


def padded_rows(activation):
    padded = padded_2(activation, (("rows", 0),), 1)
    return jnp.pad(padded, ((0, 0), (1, 1), (0, 0)))


def window_at(padded, position, height, columns, first_channel, depth):
    tap_row = position // 3
    tap_col = position % 3
    window = padded[
        tap_row : tap_row + height,
        tap_col : tap_col + columns,
        first_channel : first_channel + depth,
    ]
    return window.reshape(height * columns, depth)


def reorder_whole(gathered, channels):
    devices, taps, blocks, length = gathered.shape
    split = jnp.transpose(gathered, (1, 2, 0, 3))
    return split.reshape(3, 3 * channels, channels)


def gather_dense(shard, axis):
    devices = lax.axis_size(axis)
    if devices & (devices - 1):
        return lax.all_gather(shard, axis, axis=0, tiled=False)
    index = lax.axis_index(axis)
    gathered = shard[None]
    bit = devices // 2
    while bit:
        other = lax.ppermute(gathered, axis, [(i, i ^ bit) for i in range(devices)])
        gathered = jnp.concatenate([gathered, other], axis=0)
        bit //= 2
    order = [0]
    bit = devices // 2
    while bit:
        order = order + [i ^ bit for i in order]
        bit //= 2
    place = jnp.array([order.index(i) for i in range(devices)], jnp.int32)
    return jnp.take(gathered, place[jnp.arange(devices) ^ index], axis=0)


def whole_weights(kernel, channels):
    dense = jnp.transpose(kernel, (1, 0, 2))
    return reorder_whole(gather_dense(dense, "dp"), channels)


def convolve_whole(activation, weights):
    height, columns, channels = activation.shape
    padded = padded_rows(activation)
    accumulated = jnp.zeros((height * columns, channels), jnp.float32)
    for tap_row in range(3):
        windows = jnp.concatenate(
            [
                window_at(padded, 3 * tap_row + tap_col, height, columns, 0, channels)
                for tap_col in range(3)
            ],
            axis=1,
        )
        accumulated = accumulated + jnp.dot(
            windows, weights[tap_row], preferred_element_type=jnp.float32
        )
    return accumulated.reshape(height, columns, channels)


def shards(
    latents,
    mean_one,
    rstd_one,
    gain_one,
    shift_one,
    kernel_one,
    bias_one,
    embed_bias,
    mean_two,
    rstd_two,
    gain_two,
    shift_two,
    kernel_two,
    bias_two,
):
    channels = latents.shape[3]
    sample = latents[0].astype(jnp.float32)
    first_act = norm_silu(sample, mean_one, rstd_one, gain_one, shift_one).astype(jnp.bfloat16)
    hidden = (
        convolve_whole(first_act, whole_weights(kernel_one, channels)) + bias_one + embed_bias[0]
    )
    second_act = norm_silu(hidden, mean_two, rstd_two, gain_two, shift_two).astype(jnp.bfloat16)
    result = convolve_whole(second_act, whole_weights(kernel_two, channels)) + bias_two + sample
    return result.astype(jnp.bfloat16)[None]


def solution(mesh):
    placed = (
        P("dp", "rows", None, None),
        P("dp", None),
        P("dp", None),
        P(),
        P(),
        P(None, None, "dp"),
        P(),
        P("dp", None),
        P("dp", None),
        P("dp", None),
        P(),
        P(),
        P(None, None, "dp"),
        P(),
    )
    return jax.shard_map(
        shards, mesh=mesh, in_specs=placed, out_specs=P("dp", "rows", None, None), check_vma=False
    )
```

```python
import functools

import jax
import jax.numpy as jnp
from jax import lax
from jax.experimental import pallas as pl
from jax.experimental.pallas import tpu as pltpu
from jax.sharding import PartitionSpec as P

F32 = jnp.float32
BF16 = jnp.bfloat16
TAPS = 9
SLAB = 16


def padded_2(array, sides, width):
    for axis, dim in sides:
        devices, length = (lax.axis_size(axis), array.shape[dim])
        up = [(i, (i + 1) % devices) for i in range(devices - 1)]
        down = [(j, i) for i, j in up]
        last = lax.slice_in_dim(array, length - width, length, axis=dim)
        first = lax.slice_in_dim(array, 0, width, axis=dim)
        before = lax.ppermute(last, axis, up)
        after = lax.ppermute(first, axis, down)
        array = jnp.concatenate([before, array, after], axis=dim)
    return array


def norm_silu(values, group_mean, group_rstd, gain_vec, shift_vec):
    height, columns, channels = values.shape
    groups = group_mean.shape[-1]
    grouped = values.reshape(height, columns, groups, channels // groups)
    scaled = (grouped - group_mean[0][:, None]) * group_rstd[0][:, None]
    return jax.nn.silu(scaled.reshape(height, columns, channels) * gain_vec + shift_vec)


def padded_rows(activation):
    padded = padded_2(activation, (("rows", 0),), 1)
    return jnp.pad(padded, ((0, 0), (1, 1), (0, 0)))


def window_at(padded, position, height, columns, first_channel, depth):
    tap_row = position // 3
    tap_col = position % 3
    window = padded[
        tap_row : tap_row + height,
        tap_col : tap_col + columns,
        first_channel : first_channel + depth,
    ]
    return window.reshape(height * columns, depth)


def reorder_whole(gathered, channels):
    devices, taps, blocks, length = gathered.shape
    split = jnp.transpose(gathered, (1, 2, 0, 3))
    return split.reshape(3, 3 * channels, channels)


def gather_dense(shard, axis):
    devices = lax.axis_size(axis)
    if devices & (devices - 1):
        return lax.all_gather(shard, axis, axis=0, tiled=False)
    index = lax.axis_index(axis)
    gathered = shard[None]
    bit = devices // 2
    while bit:
        other = lax.ppermute(gathered, axis, [(i, i ^ bit) for i in range(devices)])
        gathered = jnp.concatenate([gathered, other], axis=0)
        bit //= 2
    order = [0]
    bit = devices // 2
    while bit:
        order = order + [i ^ bit for i in order]
        bit //= 2
    place = jnp.array([order.index(i) for i in range(devices)], jnp.int32)
    return jnp.take(gathered, place[jnp.arange(devices) ^ index], axis=0)


def whole_weights(kernel, channels):
    dense = jnp.transpose(kernel, (1, 0, 2))
    return reorder_whole(gather_dense(dense, "dp"), channels)


def convolve_whole(activation, weights):
    height, columns, channels = activation.shape
    padded = padded_rows(activation)
    accumulated = jnp.zeros((height * columns, channels), jnp.float32)
    for tap_row in range(3):
        windows = jnp.concatenate(
            [
                window_at(padded, 3 * tap_row + tap_col, height, columns, 0, channels)
                for tap_col in range(3)
            ],
            axis=1,
        )
        accumulated = accumulated + jnp.dot(
            windows, weights[tap_row], preferred_element_type=jnp.float32
        )
    return accumulated.reshape(height, columns, channels)


def shards(
    latents,
    mean_one,
    rstd_one,
    gain_one,
    shift_one,
    kernel_one,
    bias_one,
    embed_bias,
    mean_two,
    rstd_two,
    gain_two,
    shift_two,
    kernel_two,
    bias_two,
):
    channels = latents.shape[3]
    sample = latents[0].astype(jnp.float32)
    first_act = norm_silu(sample, mean_one, rstd_one, gain_one, shift_one).astype(jnp.bfloat16)
    hidden = (
        convolve_whole(first_act, whole_weights(kernel_one, channels)) + bias_one + embed_bias[0]
    )
    second_act = norm_silu(hidden, mean_two, rstd_two, gain_two, shift_two).astype(jnp.bfloat16)
    result = convolve_whole(second_act, whole_weights(kernel_two, channels)) + bias_two + sample
    return result.astype(jnp.bfloat16)[None]


def call(body, out_shapes, moved, flops=0, scratch=()):
    return pl.pallas_call(
        body,
        out_shape=out_shapes,
        scratch_shapes=list(scratch),
        cost_estimate=pl.CostEstimate(flops=flops, bytes_accessed=moved, transcendentals=0),
        compiler_params=pltpu.CompilerParams(vmem_limit_bytes=48 << 20),
    )


def prepare_body(width, first_ref, second_ref, first_out, second_out):
    half = lax.axis_index("rows")
    blocks = second_out.shape[1]
    for which in range(2):

        @pl.when(half == which)
        def _():
            for step in range(first_out.shape[2] // width):
                source = (2 * step + which) * width
                first_out[:, :, step * width : (step + 1) * width] = first_ref[
                    :, :, source : source + width
                ]
            second_out[...] = second_ref[:, which * blocks : (which + 1) * blocks, :]


def merge_body(*refs):
    out_ref = refs[-1]
    depth = refs[0].shape[1]
    for place, ref in enumerate(refs[:-1]):
        out_ref[:, place * depth : (place + 1) * depth, :] = ref[...]


def selection(steps, span, far, copies, channels):
    blocks = channels // span
    group = 4 * far * blocks
    tail = copies * group
    columns = (steps - 1) * group + tail
    row = lax.broadcasted_iota(jnp.int32, (channels, columns), 0)
    column = lax.broadcasted_iota(jnp.int32, (1, columns), 1)
    step = jnp.minimum(column // group, steps - 1)
    within = column % group
    near = within // (far * blocks)
    place = (within // blocks) % far
    block = within % blocks
    other = place * 4 + (near % 2) * 2 + near // 2
    device = jnp.bitwise_xor(lax.axis_index("dp"), other)
    source = block * span + device * steps + step
    return jnp.where(row == source, 1.0, 0.0).astype(BF16)


def silu(values):
    return values / (1.0 + jnp.exp(-values))


def store_slabs(out_ref, row, values):
    slabs = values.shape[0]
    out_ref[row, 1 : slabs + 1] = values.astype(BF16)
    zero = jnp.zeros((1, values.shape[2]), F32)
    before = jnp.concatenate([zero, values[slabs - 1, :-1]], axis=0)
    after = jnp.concatenate([values[0, 1:], zero], axis=0)
    out_ref[row, 0] = before.astype(BF16)
    out_ref[row, slabs + 1] = after.astype(BF16)


def first_body(steps, span, mine_ref, other_ref, norm_ref, out_ref, turned_ref):
    half = lax.axis_index("rows")
    local, channels, columns = mine_ref.shape
    slabs = columns // SLAB
    height = 2 * local
    select = selection(steps, span, 4, 2, channels)
    width = select.shape[1]
    padding = jnp.zeros((-channels % 128, columns), F32)
    edge = jnp.zeros(out_ref.shape[1:], BF16)
    out_ref[0] = edge
    out_ref[height + 1] = edge
    mean, rstd = norm_ref[0:1, :], norm_ref[1:2, :]
    gain, shift = norm_ref[2:3, :], norm_ref[3:4, :]
    for source, base in ((mine_ref, half * local), (other_ref, (1 - half) * local)):
        for row in range(local):
            wide = jnp.concatenate([source[row].astype(F32), padding], axis=0)
            sample = wide.T[:, :channels]
            value = ((sample - mean) * rstd) * gain + shift
            value = jnp.concatenate([silu(value), wide.T[:, channels:]], axis=1)
            for tile in range(turned_ref.shape[0]):
                turned_ref[tile] = value[:, tile * 128 : (tile + 1) * 128]
            active = jnp.concatenate(
                [
                    jnp.concatenate(
                        [
                            turned_ref[tile, pl.ds(slab, SLAB, stride=slabs), :]
                            for slab in range(slabs)
                        ],
                        axis=0,
                    )
                    for tile in range(turned_ref.shape[0])
                ],
                axis=1,
            )[:, :channels].astype(BF16)
            ordered = jnp.dot(active, select, preferred_element_type=F32)
            store_slabs(out_ref, base + row + 1, ordered.reshape(slabs, SLAB, width))


def window(ref, first, rows, slabs, tap, low, high):
    tap_row, tap_col = tap // 3, tap % 3
    block = ref[pl.ds(first + tap_row, rows), tap_col : tap_col + slabs, :, low:high]
    return block.reshape(rows * slabs * SLAB, high - low)


def tails(ref, first, rows, slabs, low, group):
    copies = 128 // group
    lane = lax.broadcasted_iota(jnp.int32, (1, 128), 1) // group
    pieces = []
    for start in range(0, TAPS, copies):
        taps = range(start, min(start + copies, TAPS))
        piece = window(ref, first, rows, slabs, start, low, low + 128)
        for position, tap in enumerate(taps):
            if position:
                piece = jnp.where(
                    lane >= position, window(ref, first, rows, slabs, tap, low, low + 128), piece
                )
        pieces.append(piece[:, : len(taps) * group])
    return jnp.concatenate(pieces, axis=1)


def place_weights(gathered, main_ref, tail_ref, steps, width):
    depth = gathered[0].shape[1]
    group = depth * len(gathered)
    for near, ref in enumerate(gathered):
        for step in range(steps):
            part = ref[:, :, step * width : (step + 1) * width]
            if step < steps - 1:
                low = step * group + near * depth
                main_ref[:, low : low + depth, :] = part
            else:
                tail_ref[:, near * depth : (near + 1) * depth, :] = part


def convolve(ref, main_ref, tail_ref, first, rows):
    slabs = ref.shape[1] - 2
    main = main_ref.shape[1]
    group = tail_ref.shape[1]
    total = None
    for tap in range(TAPS):
        part = jnp.dot(
            window(ref, first, rows, slabs, tap, 0, main),
            main_ref[tap],
            preferred_element_type=F32,
        )
        total = part if total is None else total + part
    tail = tail_ref[...].reshape(TAPS * group, tail_ref.shape[2])
    return total + jnp.dot(
        tails(ref, first, rows, slabs, main, group), tail, preferred_element_type=F32
    )


def middle_body(
    steps, span, act_ref, a_ref, b_ref, c_ref, d_ref, norm_ref, out_ref, main_ref, tail_ref
):
    height = act_ref.shape[0] - 2
    slabs = act_ref.shape[1] - 2
    width = main_ref.shape[2]
    place_weights((a_ref, b_ref, c_ref, d_ref), main_ref, tail_ref, steps, width)
    select = selection(steps, span, 4, out_ref.shape[3] // 128 * 2, width)
    edge = jnp.zeros(out_ref.shape[1:], BF16)
    out_ref[0] = edge
    out_ref[height + 1] = edge
    hidden = convolve(act_ref, main_ref, tail_ref, 0, height) + norm_ref[4:5, :]
    value = ((hidden - norm_ref[0:1, :]) * norm_ref[1:2, :]) * norm_ref[2:3, :] + norm_ref[3:4, :]
    active = silu(value).astype(BF16)
    ordered = jnp.dot(active, select, preferred_element_type=F32)
    ordered = ordered.reshape(height, slabs, SLAB, select.shape[1])
    for row in range(height):
        store_slabs(out_ref, row + 1, ordered[row])


def last_body(
    steps, act_ref, a_ref, b_ref, c_ref, d_ref, bias_ref, mine_ref,
    send_ref, keep_ref, main_ref, tail_ref, turned_ref,
):
    half = lax.axis_index("rows")
    local, channels, columns = mine_ref.shape
    slabs = columns // SLAB
    width = main_ref.shape[2]
    place_weights((a_ref, b_ref, c_ref, d_ref), main_ref, tail_ref, steps, width)
    for keep in (False, True):
        first = (half if keep else 1 - half) * local
        part = convolve(act_ref, main_ref, tail_ref, first, local)
        if keep:
            part = part + bias_ref[...]
        padding = jnp.zeros((part.shape[0], -channels % 128), F32)
        part = jnp.concatenate([part, padding], axis=1).reshape(local, slabs, SLAB, -1)
        for row in range(local):
            for tile in range(turned_ref.shape[0]):
                for slab in range(slabs):
                    turned_ref[tile, pl.ds(slab, SLAB, stride=slabs), :] = part[
                        row, slab, :, tile * 128 : (tile + 1) * 128
                    ]
            turned = jnp.concatenate(
                [turned_ref[tile].T for tile in range(turned_ref.shape[0])], axis=0
            )[:channels]
            if keep:
                keep_ref[row] = turned + mine_ref[row].astype(F32)
            else:
                send_ref[row] = turned.astype(BF16)


def finish_body(keep_ref, got_ref, out_ref):
    out_ref[...] = (keep_ref[...] + got_ref[...].astype(F32)).astype(BF16)


def paired(
    latents,
    mean_one,
    rstd_one,
    gain_one,
    shift_one,
    kernel_one,
    bias_one,
    embed_bias,
    mean_two,
    rstd_two,
    gain_two,
    shift_two,
    kernel_two,
    bias_two,
):
    channels = latents.shape[3]
    local, columns = latents.shape[1], latents.shape[2]
    blocks, taps, length = kernel_one.shape
    steps = length // channels
    span = channels // blocks
    width = channels // 2
    slabs = columns // SLAB
    height = 2 * local
    devices = lax.axis_size("dp")
    half = lax.axis_index("rows")
    group_size = channels // mean_one.shape[1]
    array = jax.ShapeDtypeStruct

    def swap(value, mask):
        return lax.ppermute(value, "dp", [(i, i ^ mask) for i in range(devices)])

    def across(value):
        return lax.ppermute(value, "rows", [(0, 1), (1, 0)])

    def spread(groups):
        return jnp.repeat(groups[0], group_size)

    first, second = call(
        functools.partial(prepare_body, width),
        (
            array((taps, blocks, steps * width), BF16),
            array((taps, blocks // 2, length), BF16),
        ),
        500_000,
    )(jnp.transpose(kernel_one, (1, 0, 2)), jnp.transpose(kernel_two, (1, 0, 2)))

    mine = jnp.transpose(latents[0], (0, 2, 1))
    far = [devices // 4, devices // 2, 3 * devices // 4]
    first_far = [swap(first, mask) for mask in far]
    other = across(mine)
    second_far = [swap(second, mask) for mask in far]

    norm_one = jnp.stack([spread(mean_one), spread(rstd_one), gain_one, shift_one])
    norm_two = jnp.stack(
        [spread(mean_two), spread(rstd_two), gain_two, shift_two, bias_one + embed_bias[0]]
    )
    norm_two = lax.dynamic_slice_in_dim(norm_two, half * width, width, axis=1)

    def widen(near, parts):
        depth, lanes = near.shape[1:]
        merged = call(merge_body, array((taps, 4 * depth, lanes), BF16), 1_000_000)(near, *parts)
        beside = swap(merged, 2)
        return (merged, beside, swap(merged, 1), swap(beside, 1))

    act = call(
        functools.partial(first_body, steps, span),
        array((height + 2, slabs + 2, SLAB, 4 * 4 * blocks * (steps + 1)), BF16),
        3_000_000,
        scratch=[pltpu.VMEM((-(-channels // 128), columns, 128), F32)],
    )(mine, other, norm_one)
    first_all = widen(first, first_far)
    second_all = widen(second, second_far)
    group = 16 * blocks
    act = call(
        functools.partial(middle_body, steps, span),
        array((height + 2, slabs + 2, SLAB, (group // 2) * (steps - 1) + 128), BF16),
        5_000_000,
        flops=2 * height * columns * taps * channels * width,
        scratch=[
            pltpu.VMEM((taps, group * (steps - 1), width), BF16),
            pltpu.VMEM((taps, group, width), BF16),
        ],
    )(act, *first_all, norm_two)
    group = group // 2
    send, keep = call(
        functools.partial(last_body, steps),
        (array(mine.shape, BF16), array(mine.shape, F32)),
        5_000_000,
        flops=2 * height * columns * taps * channels * width,
        scratch=[
            pltpu.VMEM((taps, group * (steps - 1), channels), BF16),
            pltpu.VMEM((taps, group, channels), BF16),
            pltpu.VMEM((-(-channels // 128), columns, 128), F32),
        ],
    )(act, *second_all, bias_two[None], mine)
    result = call(finish_body, array(mine.shape, BF16), 1_000_000)(keep, across(send))
    return jnp.transpose(result, (0, 2, 1))[None]


def fits(mesh):
    return mesh.shape["dp"] == 16 and mesh.shape["rows"] == 2


def solution(mesh):
    placed = (
        P("dp", "rows", None, None),
        P("dp", None),
        P("dp", None),
        P(),
        P(),
        P(None, None, "dp"),
        P(),
        P("dp", None),
        P("dp", None),
        P("dp", None),
        P(),
        P(),
        P(None, None, "dp"),
        P(),
    )
    return jax.shard_map(
        paired if fits(mesh) else shards,
        mesh=mesh, in_specs=placed, out_specs=P("dp", "rows", None, None), check_vma=False
    )
```
